256 devices in a mesh: seq: 32 (over y, z), tensor: 8 (over x, core).
Axes of the slice: x: 4, y: 4, z: 8, core: 2. Of those that a mesh axis runs over, the one named last changes fastest.
Arguments:
- state: bfloat16 [32768, 2048], P('seq', 'tensor'), may hold values from -20.5 to 20.5
- memory: bfloat16 [512, 2048], P('seq', 'tensor'), may hold values from -20.5 to 20.5
- w_query: bfloat16 [2048, 2048], P('seq', 'tensor'), may hold values from -0.1875 to 0.1875
- w_key: bfloat16 [2048, 2048], P('seq', 'tensor'), may hold values from -0.1875 to 0.1875
- w_value: bfloat16 [2048, 2048], P('seq', 'tensor'), may hold values from -0.125 to 0.125
- w_output: bfloat16 [2048, 2048], P('tensor', 'seq'), may hold values from -0.375 to 0.375
- norm_gain: float32 [2048], P('tensor'), may hold values from 0.1 to 1.9
- remaining: int32 [32768], P('seq'), may hold values from 0 to 3
- slot_home: int32 [512], replicated, may hold values from 0 to 31
Outputs:
- new_state: bfloat16 [32768, 2048], P('seq', 'tensor')
- new_memory: bfloat16 [512, 2048], P('seq', 'tensor')
The draws below stay inside these ranges and needn't reach their ends.
Inputs may be any that keep to these rules, and one draw needn't show every extreme that they name: `remaining`: 0 means the token has halted.
All inputs are finite; a program needn't handle non-finite values.
Results may differ from the reference program's by a relative error of at most 0.014.
The reference program's roundings to bfloat16 on the way count: a program that leaves them out, or rounds other values in their place, can miss the bound.
Values may be sent and summed in bfloat16 or wider, within the bound.
No kernel may reach another device: no remote copies, remote signals or barrier semaphores. Data moves between devices by JAX's collectives and lax.ppermute only.
A program may use at most 128 MiB of HBM per device.

```python
import math
import jax
import jax.numpy as jnp
from jax import lax

D = 2048
H = 16
HD = 128
HALF = 256
TOK_DEV = 1024
QB = 512
SEQ = 32768
MEM = 512
N_SEQ = 32
N_TENSOR = 8


def draw_rows(key, count):
    base_key = jax.random.fold_in(key, 0)
    return jnp.clip(jax.random.normal(base_key, (count, D), jnp.float32), -5.0, 5.0)


def draw_state(key, part):
    return draw_rows(jax.random.fold_in(key, 3), SEQ).astype(jnp.bfloat16)


def draw_memory(key, part):
    return draw_rows(jax.random.fold_in(key, 7), MEM).astype(jnp.bfloat16)


def place_ends(entries, own_key, smallest, high):
    shape = entries.shape
    place = [jax.random.randint(jax.random.fold_in(own_key, axis), (), 0, shape[axis]) for axis in range(len(shape))]
    entries = entries.at[tuple(place)].set(smallest)
    longest = shape.index(max(shape))
    place[longest] = (place[longest] + 1) % shape[longest]
    return entries.at[tuple(place)].set(high)


def level_of(key, dims, cuts, smallest, largest):
    loudness = 1.0
    for axis_at, shards_of in cuts:
        steps = jax.random.uniform(jax.random.fold_in(jax.random.fold_in(key, 6), axis_at), (shards_of,), jnp.float32, smallest / len(cuts), largest / len(cuts))
        loudness = loudness * jnp.repeat(jnp.exp(steps), dims[axis_at] // shards_of).reshape((-1,) + (1,) * (len(dims) - 1 - axis_at))
    return loudness


def gaussian(own_key, dims, deviation, bound, cuts=(), kind=jnp.bfloat16):
    values = jax.random.normal(own_key, dims, jnp.float32) * deviation
    if len(cuts) > 0:
        values = level_of(own_key, dims, cuts, -0.22, 0.18) * values
    return jnp.clip(values, min=-bound, max=bound).astype(kind)


def setup_inputs(seed: int = 0) -> dict:
    key_of = jax.random.split(jax.random.key(seed), 10)
    return {
        "state": draw_state(jax.random.fold_in(key_of[9], 71), 0),
        "memory": draw_memory(jax.random.fold_in(key_of[9], 71), 0),
        "w_query": gaussian(key_of[2], (D, D), (D // 2) ** -0.5, 0.1875, ((0, 32), (1, 8))),
        "w_key": gaussian(key_of[3], (D, D), (D // 2) ** -0.5, 0.1875, ((0, 32), (1, 8))),
        "w_value": gaussian(key_of[4], (D, D), D ** -0.5, 0.125, ((0, 32), (1, 8))),
        "w_output": gaussian(key_of[5], (D, D), (D // 8) ** -0.5, 0.375, ((0, 8), (1, 32))),
        "norm_gain": jnp.clip(1.0 + 0.18 * jax.random.normal(key_of[6], (D,), jnp.float32), 0.1, 1.9),
        "remaining": place_ends(jax.random.randint(key_of[7], (SEQ,), 0, 4), jax.random.fold_in(key_of[7], 1), 0, 3).astype(jnp.int32),
        "slot_home": place_ends(jax.random.randint(key_of[8], (MEM,), 0, N_SEQ), jax.random.fold_in(key_of[8], 1), 0, N_SEQ - 1).astype(jnp.int32),
    }


EPS = 1e-05
MASKED = -1e+30

def reference(state, memory, w_query, w_key, w_value, w_output, norm_gain, remaining, slot_home):
    rows = jnp.concatenate([state, memory], axis=0)
    query = jnp.dot(rows, w_query, preferred_element_type=jnp.float32).astype(jnp.bfloat16)
    keys = jnp.dot(rows, w_key, preferred_element_type=jnp.float32).astype(jnp.bfloat16)
    values = jnp.dot(rows, w_value, preferred_element_type=jnp.float32).astype(jnp.bfloat16)
    score_scale = 1.0 / math.sqrt(HD)
    distance_slopes = 0.25 * 8.0 ** (jnp.arange(H, dtype=jnp.int32).astype(jnp.float32) / (H - 1))
    homes = slot_home.astype(jnp.float32)
    tok_query = query[:SEQ].reshape(SEQ, H, HD)
    token_key_rows = keys[:SEQ].reshape(SEQ, H, HD)
    token_value_rows = values[:SEQ].reshape(SEQ, H, HD)
    memory_slot_query = query[SEQ:].reshape(MEM, H, HD).astype(jnp.float32)
    memory_slot_keys = keys[SEQ:].reshape(MEM, H, HD).astype(jnp.float32)
    memory_slot_values = values[SEQ:].reshape(MEM, H, HD).astype(jnp.float32)
    pad_keys = jnp.pad(token_key_rows, ((HALF, HALF), (0, 0), (0, 0)))
    pad_values = jnp.pad(token_value_rows, ((HALF, HALF), (0, 0), (0, 0)))
    window_extent = QB + 2 * HALF

    def token_block(number):
        start = number * QB
        query_matrix = lax.dynamic_slice_in_dim(tok_query, start, QB, 0).astype(jnp.float32)
        near_keys = lax.dynamic_slice_in_dim(pad_keys, start, window_extent, 0).astype(jnp.float32)
        near_values = lax.dynamic_slice_in_dim(pad_values, start, window_extent, 0).astype(jnp.float32)
        near = jnp.einsum('qhd,khd->hqk', query_matrix, near_keys) * score_scale
        qpos = start + jnp.arange(QB, dtype=jnp.int32)
        kpos = start - HALF + jnp.arange(window_extent, dtype=jnp.int32)
        valid = (jnp.abs(qpos[:, None] - kpos[None, :]) <= HALF) & (kpos >= 0)[None, :] & (kpos < SEQ)[None, :]
        near = jnp.where(valid[None], near, MASKED)
        blocks = (qpos // TOK_DEV).astype(jnp.float32)
        position_distances = jnp.abs(homes[None, :] - blocks[:, None])
        distant_mask = jnp.einsum('taw,caw->atc', query_matrix, memory_slot_keys) * score_scale - distance_slopes[:, None, None] * position_distances[None]
        scores = jnp.concatenate([near, distant_mask], axis=2)
        top = lax.optimization_barrier(jnp.max(scores, axis=2, keepdims=True))
        exponent_terms = jnp.exp(scores - top)
        total = lax.optimization_barrier(jnp.sum(exponent_terms, axis=2))
        attention_probabilities = lax.optimization_barrier(exponent_terms.astype(jnp.bfloat16)).astype(jnp.float32)
        both_values = jnp.concatenate([near_values, memory_slot_values], axis=0)
        numer = jnp.einsum('hqk,khd->qhd', attention_probabilities, both_values)
        return (numer / jnp.transpose(total)[:, :, None]).astype(jnp.bfloat16).reshape(QB, D)
    token_mix = lax.map(token_block, jnp.arange(SEQ // QB, dtype=jnp.int32)).reshape(SEQ, D)

    def slot_block(carry, number):
        best, den, num = carry
        start = number * TOK_DEV
        window_block_keys = lax.dynamic_slice_in_dim(token_key_rows, start, TOK_DEV, 0).astype(jnp.float32)
        window_block_values = lax.dynamic_slice_in_dim(token_value_rows, start, TOK_DEV, 0).astype(jnp.float32)
        position_distances = jnp.abs(homes - number.astype(jnp.float32))
        unnormalized_scores = jnp.einsum('gki,pki->kgp', memory_slot_query, window_block_keys) * score_scale - distance_slopes[:, None, None] * position_distances[None, :, None]
        local = lax.optimization_barrier(jnp.max(unnormalized_scores, axis=2))
        exponent_terms = jnp.exp(unnormalized_scores - local[:, :, None])
        part_den = lax.optimization_barrier(jnp.sum(exponent_terms, axis=2))
        attention_probabilities = lax.optimization_barrier(exponent_terms.astype(jnp.bfloat16)).astype(jnp.float32)
        partial_numerator = jnp.einsum('lca,alg->lcg', attention_probabilities, window_block_values)
        new_best = jnp.maximum(best, local)
        old_weight = jnp.exp(best - new_best)
        new_weight = jnp.exp(local - new_best)
        den = old_weight * den + new_weight * part_den
        num = old_weight[:, :, None] * num + new_weight[:, :, None] * partial_numerator
        return ((new_best, den, num), None)
    start_carry = (jnp.full((H, MEM), MASKED, jnp.float32), jnp.zeros((H, MEM), jnp.float32), jnp.zeros((H, MEM, HD), jnp.float32))
    (best, den, num), unused = lax.scan(slot_block, start_carry, jnp.arange(N_SEQ, dtype=jnp.int32))
    slot_mix = jnp.transpose(num / den[:, :, None], (1, 0, 2)).astype(jnp.bfloat16).reshape(MEM, D)
    mixed = jnp.concatenate([token_mix, slot_mix], axis=0)
    group = D // N_TENSOR
    summed = jnp.zeros((SEQ + MEM, D), jnp.float32)
    for index in range(N_TENSOR):
        part = jnp.dot(mixed[:, index * group:(index + 1) * group], w_output[index * group:(index + 1) * group], preferred_element_type=jnp.float32)
        summed = summed + lax.optimization_barrier(part.astype(jnp.bfloat16)).astype(jnp.float32)
    merged = rows.astype(jnp.float32) + summed
    mean_sq = lax.optimization_barrier(jnp.mean(merged * merged, axis=1, keepdims=True))
    normalized = (merged * lax.rsqrt(mean_sq + EPS) * norm_gain[None, :]).astype(jnp.bfloat16)
    new_state = jnp.where((remaining > 0)[:, None], normalized[:SEQ], state)
    new_memory = normalized[SEQ:]
    return (new_state, new_memory)
```

```python
import functools
import math

import jax
import jax.numpy as jnp
from jax import lax
from jax.experimental import pallas as pl
from jax.experimental.pallas import tpu as pltpu
from jax.sharding import PartitionSpec as P

HD = 128
HALF = 256
H = 16
EPS = 1e-05
MASKED = -1e30
LOG2E = 1.4426950408889634
NY, NZ, NX, NC = 4, 8, 4, 2
F32 = jnp.float32
BF16 = jnp.bfloat16


def z_perm(k):
    return [(y * NZ + z, y * NZ + (z + k) % NZ) for y in range(NY) for z in range(NZ)]


def y_perm(k):
    return [(y * NZ + z, ((y + k) % NY) * NZ + z) for y in range(NY) for z in range(NZ)]


def x_perm(k):
    return [(x * NC + c, ((x + k) % NX) * NC + c) for x in range(NX) for c in range(NC)]


def core_perm():
    return [(x * NC + c, x * NC + 1 - c) for x in range(NX) for c in range(NC)]


def ring_gather(own, axis, perm, n):
    out = [None] * n
    out[0] = own
    right = left = own
    for j in range(1, n // 2):
        right = lax.ppermute(right, axis, perm(1))
        left = lax.ppermute(left, axis, perm(-1))
        out[j] = right
        out[n - j] = left
    cut = -(-own.shape[0] // 32) * 16
    upper = lax.ppermute(right[:cut], axis, perm(1))
    lower = lax.ppermute(left[cut:], axis, perm(-1))
    out[n // 2] = jnp.concatenate([upper, lower], axis=0)
    return out


def tensor_gather(own):
    mine = ring_gather(own, "tensor", x_perm, NX)
    other = [lax.ppermute(m, "tensor", core_perm()) for m in mine]
    return [a for pair in zip(mine, other) for a in pair]


def tensor_places(x, c):
    return [
        lax.rem(x - k + NX, NX) * NC + (c if d == 0 else 1 - c) for k in range(NX) for d in range(NC)
    ]


def output_weight_routes(k):
    return [
        ((4 * a + j) * 8 + b, (4 * b + (j + k) % 4) * 8 + a)
        for a in range(8)
        for j in range(4)
        for b in range(8)
    ]


def reshard_output_weight(w_output):
    seq_place = lax.axis_index("seq")
    j = lax.rem(seq_place, 4)
    got = []
    for k in range(4):
        row_block = lax.rem(j + k, 4)
        piece = lax.dynamic_slice_in_dim(w_output, row_block * 64, 64, 0)
        got.append(lax.ppermute(piece, ("seq", "tensor"), output_weight_routes(k)))
    stacked = jnp.stack(got)
    order = lax.rem(j - jnp.arange(4, dtype=jnp.int32) + 4, 4)
    return jnp.concatenate([stacked[order[q]] for q in range(4)], axis=1)


def project_kernel(place, *refs):
    xs, a_parts, b_parts = refs[:8], refs[8:12], refs[12:20]
    q_ref, k_ref, v_ref, w_ref, wo_ref = refs[20:]
    y, z, x, c = place[0], place[1], place[2], place[3]
    for dy in range(NY):
        for dz in range(NZ):
            s = lax.rem(y - dy + NY, NY) * NZ + lax.rem(z - dz + NZ, NZ)
            rows = pl.ds(pl.multiple_of(s * 64, 64), 64)
            w_ref[rows, 0:512] = a_parts[dy][dz * 80 : dz * 80 + 64, :]
            w_ref[rows, 512:768] = b_parts[dz][dy * 64 : dy * 64 + 64, 0:256]
            wo_ref[rows, :] = b_parts[dz][dy * 64 : dy * 64 + 64, 256:512]
    places = tensor_places(x, c)
    for n, out in enumerate((q_ref, k_ref, v_ref)):
        for r in range(4):
            acc = None
            for part, t in zip(xs, places):
                w = w_ref[pl.ds(pl.multiple_of(t * 256, 256), 256), n * 256 : n * 256 + 256]
                d = jnp.dot(part[r * 256 : r * 256 + 256, :], w, preferred_element_type=F32)
                acc = d if acc is None else acc + d
            out[r * 256 : r * 256 + 256, :] = acc.astype(BF16)


def slot_project_kernel(place, *refs):
    ms, w_ref = refs[:8], refs[8]
    outs = refs[9:]
    y, z, x, c = place[0], place[1], place[2], place[3]
    places = tensor_places(x, c)
    for n, out in enumerate(outs):
        for r in range(2):
            acc = None
            for part, t in zip(ms, places):
                w = w_ref[pl.ds(pl.multiple_of(t * 256, 256), 256), n * 256 : n * 256 + 256]
                d = jnp.dot(part[r * 256 : r * 256 + 256, :], w, preferred_element_type=F32)
                acc = d if acc is None else acc + d
            res = acc.astype(BF16)
            for i in range(16):
                dy, dz = divmod(r * 16 + i, NZ)
                s = lax.rem(y - dy + NY, NY) * NZ + lax.rem(z - dz + NZ, NZ)
                out[pl.ds(pl.multiple_of(s * 16, 16), 16), :] = res[i * 16 : i * 16 + 16, :]


NT = (((1,), (1,)), ((), ()))


def slot_attend_kernel(q_ref, k_ref, v_ref, bias_ref, out_ref):
    scale = LOG2E / math.sqrt(HD)
    for r in range(2):
        rows = slice(r * 256, r * 256 + 256)
        stats = []
        for h in range(2):
            cols = slice(h * HD, h * HD + HD)
            s = lax.dot_general(q_ref[rows, cols], k_ref[:, cols], NT, preferred_element_type=F32) * scale
            m = jnp.max(s, axis=1, keepdims=True)
            e = jnp.exp2(s - m)
            total = jnp.sum(e, axis=1, keepdims=True)
            num = jnp.dot(e.astype(BF16), v_ref[:, cols], preferred_element_type=F32)
            out_ref[rows, cols] = (num / total).astype(BF16)
            stats.append(m + jnp.log2(total) - bias_ref[rows, h : h + 1])
        lane = lax.broadcasted_iota(jnp.int32, (256, 128), 1)
        lse = jnp.where(lane < 64, stats[0], stats[1])
        part = lax.rem(lane, 64)
        high = lse.astype(BF16).astype(F32)
        rest = lse - high
        mid = rest.astype(BF16).astype(F32)
        low = rest - mid
        packed = jnp.where(part == 0, high, jnp.where(part == 1, mid, jnp.where(part == 2, low, 0.0)))
        out_ref[rows, 256:384] = packed.astype(BF16)


def slot_merge_kernel(in_ref, out_ref):
    stats = in_ref[:, :, 256:384].astype(F32)
    for h in range(2):
        lse = jnp.sum(stats[:, :, h * 64 : h * 64 + 64], axis=2, keepdims=True)
        top = jnp.max(lse, axis=0, keepdims=True)
        w = jnp.exp2(lse - top)
        mix = in_ref[:, :, h * HD : h * HD + HD].astype(F32)
        num = jnp.sum(w * mix, axis=0)
        den = jnp.sum(w, axis=0)
        out_ref[:, h * HD : h * HD + HD] = (num / den).astype(BF16)


def token_attend_kernel(place, q_ref, k_ref, v_ref, before_ref, after_ref, sk_ref, sv_ref, bias_ref, out_ref):
    scale = LOG2E / math.sqrt(HD)
    seq_place = place[0] * NZ + place[1]
    row = lax.broadcasted_iota(jnp.int32, (256, 256), 0)
    col = lax.broadcasted_iota(jnp.int32, (256, 256), 1)
    for b in range(4):
        rows = slice(b * 256, b * 256 + 256)
        for h in range(2):
            cols = slice(h * HD, h * HD + HD)
            vcols = slice(256 + h * HD, 256 + h * HD + HD)
            q = q_ref[rows, cols]

            def near(keys):
                return lax.dot_general(q, keys, NT, preferred_element_type=F32) * scale

            if b == 0:
                pk, pv = before_ref[:, cols], before_ref[:, vcols]
                pmask = (col >= row) & (seq_place > 0)
            else:
                pk, pv = k_ref[b * 256 - 256 : b * 256, cols], v_ref[b * 256 - 256 : b * 256, cols]
                pmask = col >= row
            if b == 3:
                nk, nv = after_ref[:, cols], after_ref[:, vcols]
                nmask = (col <= row) & (seq_place < NY * NZ - 1)
            else:
                nk, nv = k_ref[b * 256 + 256 : b * 256 + 512, cols], v_ref[b * 256 + 256 : b * 256 + 512, cols]
                nmask = col <= row
            sp = jnp.where(pmask, near(pk), MASKED)
            so = near(k_ref[rows, cols])
            sn = jnp.where(nmask, near(nk), MASKED)
            sm = near(sk_ref[:, cols]) - bias_ref[h : h + 1, :]
            parts = [(sp, pv), (so, v_ref[rows, cols]), (sn, nv), (sm, sv_ref[:, cols])]
            top = jnp.max(sm, axis=1, keepdims=True)
            for s in (sp, so, sn):
                top = jnp.maximum(top, jnp.max(s, axis=1, keepdims=True))
            total = num = 0.0
            for s, v in parts:
                e = jnp.exp2(s - top)
                total = total + jnp.sum(e, axis=1, keepdims=True)
                num = num + jnp.dot(e.astype(BF16), v, preferred_element_type=F32)
            out_ref[rows, cols] = (num / total).astype(BF16)


def output_kernel(place, *refs):
    mixes, wo_ref, own_ref, out_ref = refs[:8], refs[8], refs[9], refs[10]
    places = tensor_places(place[2], place[3])
    for lo, n in ((0, 256), (256, 256), (512, 256), (768, 256), (1024, 16)):
        acc = own_ref[lo : lo + n, :].astype(F32)
        for part, t in zip(mixes, places):
            w = wo_ref[pl.ds(pl.multiple_of(t * 256, 256), 256), :]
            d = jnp.dot(part[lo : lo + n, :], w, preferred_element_type=F32)
            acc = acc + d.astype(BF16).astype(F32)
        out_ref[lo : lo + n, :] = acc


def call(kernel, outs, *args, smem=None, name=None):
    vm = pl.BlockSpec(memory_space=pltpu.VMEM)
    specs = [vm] * len(args)
    if smem is not None:
        specs = [pl.BlockSpec(memory_space=pltpu.SMEM)] + specs
        args = (smem,) + args
    return pl.pallas_call(
        kernel,
        out_shape=outs,
        in_specs=specs,
        out_specs=jax.tree.map(lambda _: vm, outs),
        name=name,
        compiler_params=pltpu.CompilerParams(vmem_limit_bytes=56 * 2**20),
    )(*args)


def shape(*dims, dtype=BF16):
    return jax.ShapeDtypeStruct(dims, dtype)


def shards(state, memory, w_query, w_key, w_value, w_output, norm_gain, remaining, slot_home):
    s_place = lax.axis_index("seq")
    t_place = lax.axis_index("tensor")
    place = jnp.stack([s_place // NZ, s_place % NZ, t_place // NC, t_place % NC]).astype(jnp.int32)
    order = (t_place * 2 + jnp.arange(2, dtype=jnp.int32)).astype(F32)
    slopes = 0.25 * 8.0 ** (order / (H - 1))
    gap = jnp.abs(slot_home.astype(F32) - s_place.astype(F32))
    bias = slopes[:, None] * gap[None, :] * LOG2E

    rows = jnp.concatenate([state, memory], axis=0)
    wo_own = reshard_output_weight(w_output)
    a_own = jnp.concatenate(
        [jnp.concatenate([w_query, w_key], axis=1), jnp.pad(memory, ((0, 0), (0, 256)))], axis=0
    )
    b_own = jnp.concatenate([w_value, wo_own], axis=1)
    xs = tensor_gather(rows)
    a_parts = ring_gather(jnp.concatenate(ring_gather(a_own, "seq", z_perm, NZ), axis=0), "seq", y_perm, NY)
    b_parts = ring_gather(jnp.concatenate(ring_gather(b_own, "seq", y_perm, NY), axis=0), "seq", z_perm, NZ)

    mem_own = jnp.concatenate(
        [a.reshape(NZ, 80, 512)[:, 64:, :256].reshape(128, 256) for a in a_parts], axis=0
    )
    q, k, v, w_all, wo_all = call(
        project_kernel,
        (shape(1024, 256), shape(1024, 256), shape(1024, 256), shape(2048, 768), shape(2048, 256)),
        *xs, *a_parts, *b_parts, smem=place, name="project",
    )
    ms = tensor_gather(mem_own)
    sq, sk, sv = call(
        slot_project_kernel, (shape(512, 256),) * 3, *ms, w_all, smem=place, name="slot_project"
    )
    last = jnp.concatenate([k[768:], v[768:]], axis=1)
    initial = jnp.concatenate([k[:256], v[:256]], axis=1)
    up = [(i, i + 1) for i in range(NY * NZ - 1)]
    before = lax.ppermute(last, "seq", up)
    after = lax.ppermute(initial, "seq", [(j, i) for i, j in up])

    part = call(slot_attend_kernel, shape(512, 384), sq, k, v, bias.T, name="slot_attend")
    swapped = lax.all_to_all(part, "seq", 0, 0, tiled=True)
    slot_mix = call(slot_merge_kernel, shape(16, 256), swapped.reshape(32, 16, 384), name="slot_merge")
    token_mix = call(
        token_attend_kernel, shape(1024, 256), q, k, v, before, after, sk, sv, bias, smem=place, name="attend"
    )
    mixes = tensor_gather(jnp.concatenate([token_mix, slot_mix], axis=0))
    merged = call(output_kernel, shape(1040, 256, dtype=F32), *mixes, wo_all, rows, smem=place, name="output")
    squares = jnp.sum(merged * merged, axis=1)
    squares = squares + lax.ppermute(squares, "tensor", core_perm())
    squares = squares + (
        lax.ppermute(squares, "tensor", x_perm(1))
        + lax.ppermute(squares, "tensor", x_perm(-1))
        + lax.ppermute(squares, "tensor", x_perm(2))
    )
    normed = (merged * lax.rsqrt(squares / 2048.0 + EPS)[:, None] * norm_gain[None, :]).astype(BF16)
    new_state = jnp.where((remaining > 0)[:, None], normed[:1024], state)
    return new_state, normed[1024:]


def solution(mesh):
    placed = (
        P("seq", "tensor"), P("seq", "tensor"), P("seq", "tensor"), P("seq", "tensor"), P("seq", "tensor"),
        P("tensor", "seq"), P("tensor"), P("seq"), P(),
    )
    return jax.shard_map(
        shards,
        mesh=mesh,
        in_specs=placed,
        out_specs=(P("seq", "tensor"), P("seq", "tensor")),
        check_vma=False,
    )
```

```python
import math

import jax
import jax.numpy as jnp
from jax import lax
from jax.experimental import pallas as pl
from jax.experimental.pallas import tpu as pltpu
from jax.sharding import PartitionSpec as P


HD = 128
H = 16
EPS = 1e-05
MASKED = -1e30
LOG2E = 1.4426950408889634
NY, NZ, NX, NC = 4, 8, 4, 2
F32 = jnp.float32
BF16 = jnp.bfloat16

Z_GROUPS = [[y * NZ + z for z in range(NZ)] for y in range(NY)]


def z_perm(k):
    return [(y * NZ + z, y * NZ + (z + k) % NZ) for y in range(NY) for z in range(NZ)]


def y_perm(k):
    return [(y * NZ + z, ((y + k) % NY) * NZ + z) for y in range(NY) for z in range(NZ)]


def x_perm(k):
    return [(x * NC + c, ((x + k) % NX) * NC + c) for x in range(NX) for c in range(NC)]


def core_perm():
    return [(x * NC + c, x * NC + 1 - c) for x in range(NX) for c in range(NC)]


def ring_gather(own, axis, perm, n):
    out = [None] * n
    out[0] = own
    right = left = own
    for j in range(1, n // 2):
        right = lax.ppermute(right, axis, perm(1))
        left = lax.ppermute(left, axis, perm(-1))
        out[j] = right
        out[n - j] = left
    cut = -(-own.shape[0] // 32) * 16
    upper = lax.ppermute(right[:cut], axis, perm(1))
    lower = lax.ppermute(left[cut:], axis, perm(-1))
    out[n // 2 : n // 2 + 1] = [upper, lower]
    return out


def direct_gather(own, axis, perm, n):
    return [own] + [lax.ppermute(own, axis, perm(k)) for k in range(1, n)]


def swap_gather(own, axis, groups):
    count = len(groups[0]) if groups else lax.axis_size(axis)
    return lax.all_to_all(
        jnp.tile(own, (count, 1)), axis, 0, 0, tiled=True, axis_index_groups=groups
    )


def swap(copies, axis, groups):
    return lax.all_to_all(copies, axis, 0, 0, tiled=True, axis_index_groups=groups)


def tensor_gather(own):
    mine = direct_gather(own, "tensor", x_perm, NX)
    other = [lax.ppermute(m, "tensor", core_perm()) for m in mine]
    return [a for pair in zip(mine, other) for a in pair]


def own_place():
    s, t = lax.axis_index("seq"), lax.axis_index("tensor")
    return s // NZ, lax.rem(s, NZ), t // NC, lax.rem(t, NC)


def tensor_places(x, c):
    return [
        lax.rem(x - k + NX, NX) * NC + (c if d == 0 else 1 - c) for k in range(NX) for d in range(NC)
    ]


def output_weight_routes(k):
    return [
        ((4 * a + j) * 8 + b, (4 * b + (j + k) % 4) * 8 + a)
        for a in range(8)
        for j in range(4)
        for b in range(8)
    ]


def split_output_kernel(w_ref, *outs):
    j = lax.rem(lax.axis_index("seq"), 4)
    for k, out in enumerate(outs):
        out[...] = w_ref[pl.ds(pl.multiple_of(lax.rem(j + k, 4) * 64, 64), 64), :]


def join_output_kernel(*refs):
    parts, out_ref = refs[:4], refs[4]
    j = lax.rem(lax.axis_index("seq"), 4)
    for q in range(4):
        k = lax.rem(j - q + 4, 4)
        piece = parts[0][...]
        for i in range(1, 4):
            piece = jnp.where(k == i, parts[i][...], piece)
        out_ref[:, q * 64 : q * 64 + 64] = piece


def reshard_output_weight(w_output):
    pieces = call(split_output_kernel, (shape(64, 64),) * 4, w_output)
    got = [lax.ppermute(piece, ("seq", "tensor"), output_weight_routes(k)) for k, piece in enumerate(pieces)]
    return call(join_output_kernel, shape(64, 256), *got)


def pack_kernel(q_ref, k_ref, v_ref, m_ref, out_ref):
    for n, ref in enumerate((q_ref, k_ref, v_ref)):
        out_ref[0:64, n * 256 : n * 256 + 256] = ref[...]
    out_ref[64:80, 0:256] = m_ref[...]
    out_ref[64:80, 256:768] = jnp.zeros((16, 512), BF16)


def stack_kernel(*refs):
    parts, w_ref, m_ref = refs[:4], refs[4], refs[5]
    for i, part in enumerate(parts):
        w_ref[i * 64 : i * 64 + 64, :] = part[0:64, :]
        rows = part[64:80, 0:256]
        for n in range(NZ):
            m_ref[n * 64 + i * 16 : n * 64 + i * 16 + 16, :] = rows


def project_kernel(*refs):
    x_ref, parts = refs[0], refs[1:10]
    outs, w_ref, first_ref, last_ref = refs[10:13], refs[13], refs[14], refs[15]
    y, z, _, _ = own_place()
    for dy in range(NY):
        for dz in range(NZ):
            s = lax.rem(y - dy + NY, NY) * NZ + lax.rem(z - dz + NZ, NZ)
            part, at = (parts[dz + (dz > 4)], dy) if dz != 4 else (parts[4 + dy // 2], dy % 2)
            w_ref[pl.ds(pl.multiple_of(s * 64, 64), 64), :] = part[at * 64 : at * 64 + 64, :]

    @pl.loop(0, 4)
    def _(r):
        rows = pl.ds(pl.multiple_of(r * 256, 256), 256)
        for n, out in enumerate(outs):
            w = w_ref[:, n * 256 : n * 256 + 256]
            out[rows, :] = jnp.dot(x_ref[rows, :], w, preferred_element_type=F32).astype(BF16)

    for n, out in enumerate(outs[1:]):
        first_ref[:, n * 256 : n * 256 + 256] = out[0:256, :]
        last_ref[:, n * 256 : n * 256 + 256] = out[768:1024, :]


def slot_project_kernel(m_ref, w_ref, q_ref, k_ref, v_ref):
    y = own_place()[0]

    @pl.loop(0, 2)
    def _(r):
        x = m_ref[pl.ds(pl.multiple_of(r * 256, 256), 256), :]
        for n, out in enumerate((q_ref, k_ref, v_ref)):
            res = jnp.dot(x, w_ref[:, n * 256 : n * 256 + 256], preferred_element_type=F32).astype(BF16)
            for i in range(16):
                z, dy = divmod(i, NY)
                s = lax.rem(y - dy + NY, NY) * NZ + z + 4 * r
                out[pl.ds(pl.multiple_of(s * 16, 16), 16), :] = res[i * 16 : i * 16 + 16, :]


NT = (((1,), (1,)), ((), ()))


def slot_attend_kernel(q_ref, k_ref, v_ref, bias_ref, out_ref):
    scale = LOG2E / math.sqrt(HD)
    for r in range(2):
        rows = slice(r * 256, r * 256 + 256)
        stats = []
        for h in range(2):
            cols = slice(h * HD, h * HD + HD)
            s = lax.dot_general(q_ref[rows, cols], k_ref[:, cols], NT, preferred_element_type=F32) * scale
            m = jnp.max(s, axis=1, keepdims=True)
            e = jnp.exp2(s - m)
            total = jnp.sum(e, axis=1, keepdims=True)
            num = jnp.dot(e.astype(BF16), v_ref[:, cols], preferred_element_type=F32)
            out_ref[rows, cols] = (num / total).astype(BF16)
            stats.append(m + jnp.log2(total) - bias_ref[rows, h : h + 1])
        lane = lax.broadcasted_iota(jnp.int32, (256, 128), 1)
        lse = jnp.where(lane < 64, stats[0], stats[1])
        part = lax.rem(lane, 64)
        high = lse.astype(BF16).astype(F32)
        rest = lse - high
        mid = rest.astype(BF16).astype(F32)
        low = rest - mid
        packed = jnp.where(part == 0, high, jnp.where(part == 1, mid, jnp.where(part == 2, low, 0.0)))
        out_ref[rows, 256:384] = packed.astype(BF16)


def slot_merge_kernel(in_ref, out_ref):
    stats = in_ref[:, :, 256:384].astype(F32)
    for h in range(2):
        lse = jnp.sum(stats[:, :, h * 64 : h * 64 + 64], axis=2, keepdims=True)
        top = jnp.max(lse, axis=0, keepdims=True)
        w = jnp.exp2(lse - top)
        mix = in_ref[:, :, h * HD : h * HD + HD].astype(F32)
        num = jnp.sum(w * mix, axis=0)
        den = jnp.sum(w, axis=0)
        out_ref[:, h * HD : h * HD + HD] = (num / den).astype(BF16)


def token_attend_kernel(q_ref, k_ref, v_ref, before_ref, after_ref, sk_ref, sv_ref, bias_ref, out_ref):
    scale = LOG2E / math.sqrt(HD)
    seq_place = lax.axis_index("seq")
    row = lax.broadcasted_iota(jnp.int32, (256, 256), 0)
    col = lax.broadcasted_iota(jnp.int32, (256, 256), 1)
    for b in range(4):
        rows = slice(b * 256, b * 256 + 256)
        for h in range(2):
            cols = slice(h * HD, h * HD + HD)
            vcols = slice(256 + h * HD, 256 + h * HD + HD)
            q = q_ref[rows, cols]

            def near(keys):
                return lax.dot_general(q, keys, NT, preferred_element_type=F32) * scale

            if b == 0:
                pk, pv = before_ref[:, cols], before_ref[:, vcols]
                pmask = (col >= row) & (seq_place > 0)
            else:
                pk, pv = k_ref[b * 256 - 256 : b * 256, cols], v_ref[b * 256 - 256 : b * 256, cols]
                pmask = col >= row
            if b == 3:
                nk, nv = after_ref[:, cols], after_ref[:, vcols]
                nmask = (col <= row) & (seq_place < NY * NZ - 1)
            else:
                nk, nv = k_ref[b * 256 + 256 : b * 256 + 512, cols], v_ref[b * 256 + 256 : b * 256 + 512, cols]
                nmask = col <= row
            sp = jnp.where(pmask, near(pk), MASKED)
            so = near(k_ref[rows, cols])
            sn = jnp.where(nmask, near(nk), MASKED)
            sm = near(sk_ref[:, cols]) - bias_ref[h : h + 1, :]
            parts = [(sp, pv), (so, v_ref[rows, cols]), (sn, nv), (sm, sv_ref[:, cols])]
            top = jnp.max(sm, axis=1, keepdims=True)
            for s in (sp, so, sn):
                top = jnp.maximum(top, jnp.max(s, axis=1, keepdims=True))
            total = num = 0.0
            for s, v in parts:
                e = jnp.exp2(s - top)
                total = total + jnp.sum(e, axis=1, keepdims=True)
                num = num + jnp.dot(e.astype(BF16), v, preferred_element_type=F32)
            out_ref[rows, cols] = (num / total).astype(BF16)


def output_kernel(*refs):
    place = own_place()
    mixes, wo_ref, own_ref, out_ref, sq_ref = refs[:8], refs[8], refs[9], refs[10], refs[11]
    places = tensor_places(place[2], place[3])

    @pl.loop(0, out_ref.shape[0] // 256)
    def _(r):
        rows = pl.ds(pl.multiple_of(r * 256, 256), 256)
        acc = own_ref[rows, :].astype(F32)
        for part, t in zip(mixes, places):
            w = wo_ref[pl.ds(pl.multiple_of(t * 256, 256), 256), :]
            d = jnp.dot(part[rows, :], w, preferred_element_type=F32)
            acc = acc + d.astype(BF16).astype(F32)
        out_ref[rows, :] = acc
        squares = row_squares(acc)
        sq_ref[pl.ds(2 * r, 1), :] = squares[:, :128]
        sq_ref[pl.ds(2 * r + 1, 1), :] = squares[:, 128:]


def row_squares(acc):
    sq = acc * acc
    return jnp.sum(jnp.transpose(sq[:, :128] + sq[:, 128:]), axis=0, keepdims=True)


def slot_output_kernel(mix_ref, wo_ref, own_ref, sq_ref, out_ref, all_ref):
    acc = own_ref[...].astype(F32)
    for t in range(NX * NC):
        d = jnp.dot(
            mix_ref[t * 16 : t * 16 + 16, :], wo_ref[t * 256 : t * 256 + 256, :], preferred_element_type=F32
        )
        acc = acc + d.astype(BF16).astype(F32)
    out_ref[...] = acc
    padded = jnp.concatenate([acc, jnp.zeros((112, 256), F32)], axis=0)
    slots = jnp.broadcast_to(row_squares(padded), (8, 128))
    for t in range(NX * NC):
        all_ref[t, 0:8, :] = sq_ref[...]
        all_ref[t, 8:16, :] = slots


def call(kernel, outs, *args, scratch=()):
    vm = pl.BlockSpec(memory_space=pltpu.VMEM)
    specs = [vm] * len(args)
    return pl.pallas_call(
        kernel,
        out_shape=outs,
        in_specs=specs,
        out_specs=jax.tree.map(lambda _: vm, outs),
        scratch_shapes=scratch,
        compiler_params=pltpu.CompilerParams(vmem_limit_bytes=56 * 2**20),
    )(*args)


def shape(*dims, dtype=BF16):
    return jax.ShapeDtypeStruct(dims, dtype)


def slot_bias(s_place, t_place, slot_home):
    order = (t_place * 2 + jnp.arange(2, dtype=jnp.int32)).astype(F32)
    slopes = 0.25 * 8.0 ** (order / (H - 1)) * LOG2E
    gap = jnp.abs(slot_home.astype(F32) - s_place.astype(F32))
    return slopes[:, None] * gap[None, :], gap[:, None] * slopes[None, :]


def step(state, memory, w_query, w_key, w_value, w_output, norm_gain, remaining, slot_home):
    s_place = lax.axis_index("seq")
    t_place = lax.axis_index("tensor")
    bias, bias_rows = slot_bias(s_place, t_place, slot_home)
    rows = lax.all_gather(state, "tensor", axis=1, tiled=True)
    wo_own = reshard_output_weight(w_output)
    w_own = call(pack_kernel, shape(80, 768), w_query, w_key, w_value, memory)
    got = direct_gather(w_own, "seq", y_perm, NY)
    w_y, mem_y = call(stack_kernel, (shape(256, 768), shape(512, 256)), *got)
    w_parts = ring_gather(w_y, "seq", z_perm, NZ)
    mem_seq = swap(mem_y, "seq", Z_GROUPS)
    slot_rows = lax.all_gather(mem_seq, "tensor", axis=1, tiled=True)
    wo_all = lax.all_gather(wo_own, "seq", axis=0, tiled=True)

    q, k, v, w_all, initial, last = call(
        project_kernel, (shape(1024, 256),) * 3 + (shape(2048, 768),) + (shape(256, 512),) * 2, rows, *w_parts,
    )
    up = [(i, i + 1) for i in range(NY * NZ - 1)]
    before = lax.ppermute(last, "seq", up)
    after = lax.ppermute(initial, "seq", [(j, i) for i, j in up])
    sq, sk, sv = call(slot_project_kernel, (shape(512, 256),) * 3, slot_rows, w_all)
    part = call(slot_attend_kernel, shape(512, 384), sq, k, v, bias_rows)
    swapped = lax.all_to_all(part, "seq", 0, 0, tiled=True)
    token_mix = call(token_attend_kernel, shape(1024, 256), q, k, v, before, after, sk, sv, bias)
    mixes = tensor_gather(token_mix)
    slot_mix = call(slot_merge_kernel, shape(16, 256), swapped.reshape(32, 16, 384))
    slot_mixes = swap_gather(slot_mix, "tensor", None)
    merged, token_sq = call(
        output_kernel, (shape(1024, 256, dtype=F32), shape(8, 128, dtype=F32)), *mixes, wo_all, state,
    )
    slot_merged, squares = call(
        slot_output_kernel, (shape(16, 256, dtype=F32), shape(8, 16, 128, dtype=F32)), slot_mixes, wo_all, memory,
        token_sq,
    )
    squares = jnp.sum(lax.all_to_all(squares, "tensor", 0, 0, tiled=True), axis=0).reshape(2048)[:1040]
    scale = lax.rsqrt(squares / 2048.0 + EPS)[:, None]
    normed = (merged * scale[:1024] * norm_gain[None, :]).astype(BF16)
    new_state = jnp.where((remaining > 0)[:, None], normed, state)
    return new_state, (slot_merged * scale[1024:] * norm_gain[None, :]).astype(BF16)


def solution(mesh):
    placed = (
        P("seq", "tensor"), P("seq", "tensor"), P("seq", "tensor"), P("seq", "tensor"), P("seq", "tensor"),
        P("tensor", "seq"), P("tensor"), P("seq"), P(),
    )
    return jax.shard_map(
        step,
        mesh=mesh,
        in_specs=placed,
        out_specs=(P("seq", "tensor"), P("seq", "tensor")),
        check_vma=False,
    )
```
